32 devices in a mesh: flow: 2 (over x), cross: 4 (over z), depth: 4 (over y, core).
Axes of the slice: x: 2, y: 2, z: 4, core: 2. Of those that a mesh axis runs over, the one named last changes fastest.
Arguments:
- fluid_offsets: float32 [3, 2, 16, 16, 128], P(None, 'flow', 'cross', 'depth'), may hold values from 0 to 1
- source: float32 [2, 16, 16, 128], P('flow', 'cross', 'depth'), may hold values from -6 to 6
- marker_offsets: float32 [512, 16, 3, 128], P(('flow', 'cross', 'depth')), may hold values from 0 to 1
- marker_normals: float32 [512, 16, 3, 128], P(('flow', 'cross', 'depth')), may hold values from -6 to 6
- dest_tile: int32 [512, 16, 1], P(('flow', 'cross', 'depth')), may hold values from 0 to 7; in each aligned block of 256 rows (0 to 255, 256 to 511, ..., all dimensions but the last counted through in order) at most 64 rows name the same one
- cell_index: int32 [512, 16], P(('flow', 'cross', 'depth')), may hold values from 0 to 15
- grain_velocity: float32 [512, 3], P(('flow', 'cross', 'depth')), may hold values from -6 to 6
- grain_mass: float32 [512], P(('flow', 'cross', 'depth')), may hold values from 0.5 to 4
Outputs:
- pressure: float32 [2, 16, 16, 128], P('flow', 'cross', 'depth')
- velocity_out: float32 [512, 3], P(('flow', 'cross', 'depth'))
The draws below stay inside these ranges and needn't reach their ends.
Inputs may be any that keep to these rules, and one draw needn't show every extreme that they name: `dest_tile`: in the rows of one device at most 64 marker blocks name the same tile.
All inputs are finite; a program needn't handle non-finite values.
Results may differ from the reference program's by a relative error of at most 0.0003.
Values sent between devices are 32-bit elements; how exact they have to be, the bound alone decides.
A program may use at most 64 MiB of HBM per device.

```python
import math
import jax
import jax.numpy as jnp
import numpy as np
from jax import lax

CX = 1
CY = 4
CZ = 4
G_DEV = 16
MB = 16
ITERS = 4
STEPS = 2
CELLS = 16
NX = 2
NY = 16
NZ = 16
GRAINS = 512
CAP = 64
N_FLOW = 2
N_CROSS = 4
N_DEPTH = 4


def touch_ends(values, stream_key, least, high):
    dims = values.shape
    spot = [jax.random.randint(jax.random.fold_in(stream_key, axis), (), 0, dims[axis]) for axis in range(len(dims))]
    values = values.at[tuple(spot)].set(least)
    longest = dims.index(max(dims))
    spot[longest] = (spot[longest] + 1) % dims[longest]
    return values.at[tuple(spot)].set(high)


def block_levels(stream_key, shape, split, low, high):
    gain, own = 1.0, jax.random.fold_in(stream_key, 6)
    for position, parts in split:
        draws = jnp.exp(jax.random.uniform(jax.random.fold_in(own, position), (parts,), jnp.float32, low / len(split), high / len(split)))
        gain = gain * jnp.repeat(draws, shape[position] // parts).reshape([-1 if axis == position else 1 for axis in range(len(shape))])
    return gain


def assign_block(own_key, own, number, rows, amount, top, limit, slope):
    order = jax.random.permutation(own_key, amount)
    packed, ordinary = load_shares(amount, rows * top, limit, slope, True), load_shares(amount, rows * top, limit, slope, False)
    places = jnp.arange(amount)

    def named(sizes, offset_by):
        used = int((sizes > 0).sum())
        fixed = max(1, used // 4)
        moved = fixed + (places - fixed + offset_by * (used - fixed)) % max(1, amount - fixed)
        return jnp.zeros((amount,), jnp.int32).at[order[jnp.where(places < fixed, places, moved)]].set(jnp.asarray(sizes, jnp.int32))

    sizes = jnp.where(number % 4 == 0, named(packed, number // 4), named(ordinary, number - number // 4 - 1))
    mixed = jax.random.permutation(jax.random.fold_in(own, 3), amount)
    source_of, receiver = mixed[0:amount // 2 * 2:2], mixed[1:amount // 2 * 2:2]
    margin = jnp.minimum(sizes[source_of] - 1, limit - sizes[receiver]) // 2
    margin = jnp.where((source_of == order[0]) | (receiver == order[0]) | (sizes[receiver] == 0), 0, jnp.maximum(margin, 0))
    moved = jax.random.randint(jax.random.fold_in(own, 4), (amount // 2,), 0, 1 << 20) % (margin + 1)
    sizes = sizes.at[source_of].add(-moved).at[receiver].add(moved)
    items = jnp.searchsorted(jnp.cumsum(sizes), jnp.arange(rows * top), side="right").astype(jnp.int32)
    grid = items.reshape(top, rows).T
    grid = grid[jax.random.permutation(jax.random.fold_in(own, 1), rows)]
    offset_by = jax.random.randint(jax.random.fold_in(own, 2), (rows, 1), 0, top)
    return jnp.take_along_axis(grid, (jnp.arange(top)[None, :] + offset_by) % top, axis=1)


def load_shares(number_of, total, bound, skew, full):
    portions = [(1 << 20) // math.isqrt(grade ** skew) + 1 for grade in range(1, number_of + 1)]
    largest = bound if full else min(bound, max(-(-total // number_of), total * portions[0] // sum(portions)))
    least = 1 if total - largest >= number_of - 1 else 0
    given, spare = [largest] + [least] * (number_of - 1), total - largest - least * (number_of - 1)
    while spare > 0:
        movable = [i for i in range(1, number_of) if given[i] < largest] or [i for i in range(1, number_of) if given[i] < bound]
        whole, budget = sum([portions[i] for i in movable]), spare
        for i in movable:
            extra = min(bound - given[i], max(1, budget * portions[i] // whole), spare)
            given[i] = given[i] + extra
            spare = spare - extra
    return np.array(given)


def centred(own_key, dims, spread, reach, split=(), kind=jnp.bfloat16):
    drawn = spread * jax.random.normal(own_key, dims, jnp.float32)
    if split:
        drawn = drawn * block_levels(own_key, dims, split, -0.22, 0.18)
    return jnp.clip(drawn, -reach, reach).astype(kind)


def setup_inputs(seed: int = 0) -> dict:
    arg_keys = jax.random.split(jax.random.key(seed), 9)
    fluid_offsets = jnp.clip(1.0 * jax.random.uniform(arg_keys[0], (3, NX, NY, NZ, 128), jnp.float32) ** block_levels(arg_keys[0], (3, NX, NY, NZ, 128), ((1, 2), (2, 4), (3, 4)), -0.2, 0.2), 0.0, 1.0)
    source = centred(arg_keys[1], (NX, NY, NZ, 128), 1.0, 6.0, ((0, 2), (1, 4), (2, 4)), jnp.float32)
    marker_offsets = jnp.clip(1.0 * jax.random.uniform(arg_keys[2], (GRAINS, MB, 3, 128), jnp.float32) ** block_levels(arg_keys[2], (GRAINS, MB, 3, 128), ((0, 32),), -0.2, 0.2), 0.0, 1.0)
    marker_normals = centred(arg_keys[3], (GRAINS, MB, 3, 128), 1.0, 6.0, ((0, 32),), jnp.float32)
    dest_tile_keys = jax.random.split(jax.random.fold_in(arg_keys[4], 1), GRAINS * MB // (G_DEV * MB))
    dest_tile_turns = jax.random.permutation(jax.random.fold_in(arg_keys[4], 3), GRAINS * MB // (G_DEV * MB))
    dest_tile = jax.vmap(lambda own, number: assign_block(jax.random.fold_in(arg_keys[4], 2), own, number, G_DEV * MB, N_FLOW * N_CROSS, 1, CAP, 2))(dest_tile_keys, dest_tile_turns).reshape((GRAINS, MB, 1))
    cell_index = touch_ends(jax.random.randint(arg_keys[5], (GRAINS, MB), 0, CELLS), jax.random.fold_in(arg_keys[5], 1), 0, CELLS - 1).astype(jnp.int32)
    grain_velocity = centred(arg_keys[6], (GRAINS, 3), 1.0, 6.0, ((0, 32),), jnp.float32)
    grain_mass = jnp.clip(jnp.exp(math.log(4.0) - 2.0794415 * jax.random.uniform(arg_keys[7], (GRAINS,), jnp.float32) ** block_levels(arg_keys[7], (GRAINS,), ((0, 32),), -0.2, 0.2)), 0.5, 4.0)
    return {"fluid_offsets": fluid_offsets, "source": source, "marker_offsets": marker_offsets, "marker_normals": marker_normals, "dest_tile": dest_tile, "cell_index": cell_index, "grain_velocity": grain_velocity, "grain_mass": grain_mass}


NEIGHBOURS = ((0, 0, 0), (1, 0, 0), (-1, 0, 0), (0, 1, 0), (0, -1, 0), (0, 0, 1), (0, 0, -1))
STIFFEN = 0.5
STEP_TIME = 0.05
PER_PARTICLE = 1.0 / 128.0


def pair_kernel(own_off, near_off, offset, values):
    total = None
    for component in range(3):
        gap = (near_off[component] + float(offset[component]))[..., None, :] - own_off[component][..., :, None]
        total = gap * gap if total is None else total + gap * gap
    weight = jnp.exp(-total) * PER_PARTICLE
    return jnp.sum(weight * values[..., None, :], axis=-1)


def marker_weights(fluid_rows, positions):
    total = None
    for component in range(3):
        gap = fluid_rows[:, component, :, None] - positions[:, component, None, :]
        total = gap * gap if total is None else total + gap * gap
    return jnp.exp(-total) * PER_PARTICLE


def weighted(fluid_offsets, field):
    def one_slab(slab_index):
        own_off = lax.dynamic_index_in_dim(fluid_offsets, slab_index, 1, keepdims=False)
        total = jnp.zeros(field.shape[1:], jnp.float32)
        for offset in NEIGHBOURS:
            near_index = (slab_index + offset[0]) % NX
            near_off = lax.dynamic_index_in_dim(fluid_offsets, near_index, 1, keepdims=False)
            near_val = lax.dynamic_index_in_dim(field, near_index, 0, keepdims=False)
            near_off = jnp.roll(near_off, (-offset[1], -offset[2]), axis=(1, 2))
            near_val = jnp.roll(near_val, (-offset[1], -offset[2]), axis=(0, 1))
            total = total + pair_kernel(own_off, near_off, offset, near_val)
        return total
    return lax.map(one_slab, jnp.arange(NX, dtype=jnp.int32))


def reference(fluid_offsets, source, marker_offsets, marker_normals, dest_tile, cell_index, grain_velocity, grain_mass):
    cell_count = NX * NY * NZ
    rowsum = weighted(fluid_offsets, jnp.ones(source.shape, jnp.float32))
    diagonal = STIFFEN + rowsum - PER_PARTICLE

    def operate(field):
        return (STIFFEN + rowsum) * field - weighted(fluid_offsets, field)

    fluid_rows = jnp.transpose(fluid_offsets, (1, 2, 3, 0, 4)).reshape(cell_count, 3, 128)
    device_count = N_FLOW * N_CROSS * N_DEPTH
    per_device = G_DEV * MB
    grain_ids = jnp.arange(GRAINS, dtype=jnp.int32)
    depth_of = (grain_ids // G_DEV) % N_DEPTH
    tile_of = dest_tile[:, :, 0]
    flow_of = tile_of // N_CROSS
    cross_of = tile_of % N_CROSS
    local_x = cell_index // (CY * CZ)
    local_y = (cell_index // CZ) % CY
    local_z = cell_index % CZ
    global_x = flow_of * CX + local_x
    global_y = cross_of * CY + local_y
    global_z = depth_of[:, None] * CZ + local_z
    target = ((global_x * NY + global_y) * NZ + global_z).astype(jnp.int32)
    target_groups = target.reshape(device_count, per_device)
    offset_groups = marker_offsets.reshape(device_count, per_device, 3, 128)
    normal_groups = marker_normals.reshape(device_count, per_device, 3, 128)

    velocity = grain_velocity
    displace = jnp.zeros(grain_velocity.shape, jnp.float32)
    pressure = jnp.zeros(source.shape, jnp.float32)
    for step_index in range(STEPS):
        moved = jnp.repeat(displace, MB, axis=0).reshape(device_count, per_device, 3)
        speeds = jnp.repeat(velocity, MB, axis=0).reshape(device_count, per_device, 3)

        def contribute(pieces):
            targets, offsets, normals, shifted, moving = pieces
            positions = offsets + shifted[:, :, None]
            rate = normals[:, 0] * moving[:, 0, None] + normals[:, 1] * moving[:, 1, None] + normals[:, 2] * moving[:, 2, None]
            weight = marker_weights(fluid_rows[targets], positions)
            return jnp.sum(weight * rate[:, None, :], axis=-1)

        added = lax.map(contribute, (target_groups, offset_groups, normal_groups, moved, speeds))
        summed = jnp.zeros((cell_count, 128), jnp.float32).at[target.reshape(-1)].add(added.reshape(-1, 128))
        right_side = source + summed.reshape(source.shape)

        solution = pressure
        residual = right_side - operate(solution)
        precond = residual / diagonal
        direction = precond
        norm_now = jnp.sum(residual * precond)
        for iteration in range(ITERS):
            image = operate(direction)
            alpha = norm_now / jnp.sum(direction * image)
            solution = solution + alpha * direction
            residual = residual - alpha * image
            precond = residual / diagonal
            norm_next = jnp.sum(residual * precond)
            direction = precond + (norm_next / norm_now) * direction
            norm_now = norm_next
        pressure = solution
        pressure_rows = pressure.reshape(cell_count, 128)

        def push(pieces):
            targets, offsets, normals, shifted = pieces
            positions = offsets + shifted[:, :, None]
            weight = marker_weights(fluid_rows[targets], positions)
            felt = jnp.sum(weight * pressure_rows[targets][:, :, None], axis=1)
            return jnp.sum(normals * felt[:, None, :], axis=-1)

        block_force = lax.map(push, (target_groups, offset_groups, normal_groups, moved)).reshape(GRAINS, MB, 3)
        grain_force = jnp.sum(block_force, axis=1)
        velocity = velocity + STEP_TIME * grain_force / grain_mass[:, None]
        displace = displace + STEP_TIME * velocity
    return pressure, velocity
```

```python
import functools
import math

import jax
import jax.numpy as jnp
from jax import lax
from jax.experimental import pallas as pl
from jax.experimental.pallas import tpu as pltpu
from jax.sharding import PartitionSpec as P

ITERS = 4
STEPS = 2
STIFFEN = 0.5
STEP_TIME = 0.05
PER_PARTICLE = 1.0 / 128.0
SCALE = math.sqrt(math.log2(math.e))
SHIFT = math.log2(PER_PARTICLE)
MESH = pl.DeviceIdType.MESH
HIGHEST = lax.Precision.HIGHEST
CHUNK = 32
COLS = 8


def weight_of(gaps):
    total = None
    for gap in gaps:
        total = gap * gap if total is None else total + gap * gap
    return jnp.exp2(SHIFT - total)


def solve_small(gram, right):
    n = len(right)
    gram = [list(row) for row in gram]
    right = list(right)
    for i in range(n):
        inverse = 1.0 / gram[i][i]
        for j in range(i + 1, n):
            factor = gram[j][i] * inverse
            for k in range(i + 1, n):
                gram[j][k] = gram[j][k] - factor * gram[i][k]
            right[j] = right[j] - factor * right[i]
    out = [None] * n
    for i in reversed(range(n)):
        value = right[i]
        for k in range(i + 1, n):
            value = value - gram[i][k] * out[k]
        out[i] = value / gram[i][i]
    return out


def kernel(
    sizes,
    dims,
    slot_ref,
    cell_ref,
    off_ref,
    source_ref,
    geo_ref,
    start_ref,
    mass_ref,
    column_ref,
    row_ref,
    press_out,
    speed_out,
    off_group,
    off_depth,
    weights,
    geo_turned,
    shift_rows,
    normal_sums,
    give,
    take,
    krylov,
    krylov_depth,
    part_group,
    part_depth,
    off_send,
    off_recv,
    take_send,
    take_recv,
    kry_send,
    kry_recv,
    part_send,
    part_recv,
):
    n_flow, n_cross, n_depth = sizes
    size_x, size_y, size_z = dims
    cells = size_x * size_y * size_z
    tiles = n_flow * n_cross
    grains = geo_ref.shape[0]
    blocks = column_ref.shape[0]
    per_grain = blocks // grains
    lanes = off_ref.shape[-1]
    flow, cross, depth = (lax.axis_index("flow"), lax.axis_index("cross"), lax.axis_index("depth"))

    def group_at(slot):
        rf, rc = divmod(slot, n_cross)
        return (lax.rem(flow + rf, n_flow), lax.rem(cross + rc, n_cross), depth)

    def group_back(slot):
        rf, rc = divmod(slot, n_cross)
        return (
            lax.rem(flow + n_flow - rf, n_flow),
            lax.rem(cross + n_cross - rc, n_cross),
            depth,
        )

    def depth_at(rd):
        return (flow, cross, lax.rem(depth + rd, n_depth))

    slot_flow = {1: (n_flow - 1) * n_cross, -1: (1 % n_flow) * n_cross}
    slot_cross = {1: n_cross - 1, -1: 1 % n_cross}
    near_slots = sorted({slot_flow[1], slot_flow[-1], slot_cross[1], slot_cross[-1]} - {0})
    far_slots = [r for r in range(1, tiles) if r not in near_slots]
    near_slots = sorted(near_slots, key=lambda r: r // n_cross)
    order = near_slots + far_slots
    near_depth = sorted({1, n_depth - 1})
    depth_index = {1: near_depth.index(n_depth - 1), -1: near_depth.index(1)}

    barrier = pltpu.get_barrier_semaphore()
    for r in range(1, tiles):
        pl.semaphore_signal(barrier, inc=1, device_id=group_at(r), device_id_type=MESH)
    for rd in range(1, n_depth):
        pl.semaphore_signal(barrier, inc=1, device_id=depth_at(rd), device_id_type=MESH)
    pl.semaphore_wait(barrier, tiles - 1 + n_depth - 1)

    sent = []

    def ship(src, dst, send_sem, recv_sem, device):
        copy = pltpu.make_async_remote_copy(
            src_ref=src,
            dst_ref=dst,
            send_sem=send_sem,
            recv_sem=recv_sem,
            device_id=device,
            device_id_type=MESH,
        )
        copy.start()
        sent.append(copy)
        return copy

    off_copies = {}
    for r in order:
        off_copies[r] = ship(
            off_ref, off_group.at[r], off_send.at[r], off_recv.at[r], group_at(r)
        )
    off_depth_copies = []
    for i, rd in enumerate(near_depth):
        off_depth_copies.append(
            ship(
                off_ref,
                off_depth.at[i],
                off_send.at[tiles + i],
                off_recv.at[tiles + i],
                depth_at(rd),
            )
        )
    off_group[0] = off_ref[...]

    def turn(g, carry):
        geo_turned[g] = jnp.transpose(geo_ref[g])
        return carry

    lax.fori_loop(0, grains, turn, 0)
    for r in order:
        off_copies[r].wait_recv()

    one_hot_row = (
        lax.broadcasted_iota(jnp.int32, (tiles * cells, blocks), 0) == row_ref[...]
    ).astype(jnp.float32)

    def marker_pass(g, carry):
        shift = shift_rows[pl.ds(g, 1), :]
        rows = [[], [], []]
        for b in range(per_grain):
            slot = slot_ref[g * per_grain + b]
            cell = cell_ref[g * per_grain + b]
            own = [off_group[slot, pl.ds(c * cells + cell, 1), :] for c in range(3)]
            sums = [None, None, None]
            for low in range(0, lanes, CHUNK):
                piece = geo_turned[g, low : low + CHUNK, :] + shift
                weight = weight_of(
                    [piece[:, b * COLS + c : b * COLS + c + 1] - own[c] for c in range(3)]
                )
                for c in range(3):
                    term = piece[:, b * COLS + 3 + c : b * COLS + 4 + c] * weight
                    term = jnp.sum(term.reshape(CHUNK // 8, 8, lanes), axis=0)
                    sums[c] = term if sums[c] is None else sums[c] + term
            for c in range(3):
                rows[c].append(jnp.sum(sums[c], axis=0, keepdims=True))
        for c in range(3):
            normal_sums[c, pl.ds(pl.multiple_of(g * per_grain, 8), per_grain), :] = jnp.concatenate(
                rows[c], axis=0
            )
        return carry

    lane = lax.rem(lax.broadcasted_iota(jnp.int32, (grains, lanes), 1), COLS)
    speed = start_ref[...]
    moved = jnp.zeros((grains, lanes), jnp.float32)
    velocity = [jnp.broadcast_to(speed[:, c : c + 1], (grains, lanes)) for c in range(3)]
    displace = [moved, moved, moved]

    def to_fluid(step):
        added = None
        for c in range(3):
            term = normal_sums[c].reshape(grains, per_grain, lanes) * velocity[c][:, None, :]
            added = term if added is None else added + term
        spread = jnp.dot(
            one_hot_row,
            added.reshape(blocks, lanes),
            precision=HIGHEST,
            preferred_element_type=jnp.float32,
        )
        give[step] = spread.reshape(tiles, cells, lanes)
        return [
            ship(
                give.at[step, r],
                take.at[step, r],
                take_send.at[step, r],
                take_recv.at[step, r],
                group_back(r),
            )
            for r in reversed(order)
        ]

    def collect(step, copies):
        total = give[step, 0]
        for copy in copies:
            copy.wait_recv()
        for r in range(1, tiles):
            total = total + take[step, r]
        return total

    merged = size_x == 1 and n_flow == 2
    sources = {("own", 0): 0}
    flow_keys = [("flow", 1)] if merged else [("flow", 1), ("flow", -1)]
    for key in flow_keys + [("cross", 1), ("cross", -1), ("depth", 1), ("depth", -1)]:
        sources[key] = len(sources)
    padded_rows = -(-len(sources) * cells // 128) * 128

    def columns_of(pick):
        rows = []
        for axis, side in sources:
            if axis == "own":
                rows.append(pick(0, None))
            elif axis == "flow":
                rows.append(pick(slot_flow[side], None))
            elif axis == "cross":
                rows.append(pick(slot_cross[side], None))
            else:
                rows.append(pick(None, depth_index[side]))
        spare = padded_rows - len(sources) * cells
        if spare:
            rows.append(jnp.zeros((spare, lanes), jnp.float32))
        return jnp.transpose(jnp.concatenate(rows, axis=0))

    def pairs(cell):
        x, rest = divmod(cell, size_y * size_z)
        y, z = divmod(rest, size_z)
        found = [(cell, (0, 0, 0))]
        place, extent, names = (x, y, z), (size_x, size_y, size_z), ("flow", "cross", "depth")
        for axis in range(3):
            for side in (1, -1):
                near = list(place)
                near[axis] += side
                key = ("own", 0)
                if not 0 <= near[axis] < extent[axis]:
                    near[axis] %= extent[axis]
                    key = (names[axis], side)
                    if axis == 0 and merged:
                        key = (names[axis], 1)
                index = (near[0] * size_y + near[1]) * size_z + near[2]
                step = [0, 0, 0]
                step[axis] = side
                found.append((sources[key] * cells + index, tuple(step)))
        return found

    groups = []
    for cell in range(cells):
        by_column = {}
        for column, step in pairs(cell):
            by_column.setdefault(column, []).append(step)
        groups.append(list(by_column.items()))

    shift_rows[...] = moved
    lax.fori_loop(0, grains, marker_pass, 0)
    copies = to_fluid(0)
    for copy in off_depth_copies:
        copy.wait_recv()

    turned = [
        columns_of(
            lambda slot, i, c=c: (
                off_group[slot, c * cells : (c + 1) * cells, :]
                if i is None
                else off_depth[i, c * cells : (c + 1) * cells, :]
            )
        )
        for c in range(3)
    ]
    sum_rows = []
    for cell in range(cells):
        own = [off_ref[c * cells + cell : c * cells + cell + 1, :] for c in range(3)]
        full = None
        for position, (column, steps) in enumerate(groups[cell]):
            total = None
            for step in steps:
                weight = weight_of(
                    [
                        turned[c][:, column : column + 1] - (own[c] - SCALE * step[c])
                        for c in range(3)
                    ]
                )
                total = weight if total is None else total + weight
            weights[cell, position] = total
            full = total if full is None else full + total
        sum_rows.append(jnp.sum(full, axis=0, keepdims=True))
    rowsum = jnp.concatenate(sum_rows, axis=0)
    diagonal = STIFFEN + rowsum - PER_PARTICLE
    inverse = 1.0 / diagonal

    def weighted(step, j):
        turned_field = columns_of(
            lambda slot, i: krylov[step, j, slot] if i is None else krylov_depth[step, j, i]
        )
        rows = []
        for cell in range(cells):
            total = None
            for low in range(0, lanes, 64):
                acc = None
                for position, (column, _) in enumerate(groups[cell]):
                    term = (
                        weights[cell, position, low : low + 64, :]
                        * turned_field[low : low + 64, column : column + 1]
                    )
                    acc = term if acc is None else acc + term
                acc = jnp.sum(acc.reshape(8, 8, lanes), axis=0)
                total = acc if total is None else total + acc
            rows.append(jnp.sum(total, axis=0, keepdims=True))
        return jnp.concatenate(rows, axis=0)

    pressure = jnp.zeros((cells, lanes), jnp.float32)
    spread_before = None
    residual = None
    pressure_all = None
    one_hot_column = (
        lax.broadcasted_iota(jnp.int32, (blocks, tiles * cells), 1) == column_ref[...]
    ).astype(jnp.float32)
    for step in range(STEPS):
        if step:
            shift_rows[...] = moved * SCALE
            lax.fori_loop(0, grains, marker_pass, 0)
            copies = to_fluid(step)
        spread = collect(step, copies)
        if step == 0:
            residual = source_ref[...] + spread
        else:
            residual = residual + (spread - spread_before)
        spread_before = spread
        fields = [residual * inverse]
        far = []
        for j in range(ITERS):
            krylov[step, j, 0] = fields[j]
            near = {}
            for r in near_slots:
                near[r] = ship(
                    krylov.at[step, j, 0],
                    krylov.at[step, j, r],
                    kry_send.at[step, j, r],
                    kry_recv.at[step, j, r],
                    group_at(r),
                )
            beside = [
                ship(
                    krylov.at[step, j, 0],
                    krylov_depth.at[step, j, i],
                    kry_send.at[step, j, tiles + i],
                    kry_recv.at[step, j, tiles + i],
                    depth_at(rd),
                )
                for i, rd in enumerate(near_depth)
            ]
            for r in far_slots:
                far.append(
                    ship(
                        krylov.at[step, j, 0],
                        krylov.at[step, j, r],
                        kry_send.at[step, j, r],
                        kry_recv.at[step, j, r],
                        group_at(r),
                    )
                )
            for copy in list(near.values()) + beside:
                copy.wait_recv()
            fields.append((weighted(step, j) - PER_PARTICLE * fields[j]) * inverse)
        moments = []
        for j in range(ITERS):
            scaled = diagonal * fields[j]
            moments.append(jnp.sum(scaled * fields[j], axis=0, keepdims=True))
            moments.append(jnp.sum(scaled * fields[j + 1], axis=0, keepdims=True))
        part_group[step, 0] = jnp.concatenate(moments, axis=0)
        waits = [
            ship(
                part_group.at[step, 0],
                part_group.at[step, r],
                part_send.at[step, r],
                part_recv.at[step, r],
                group_at(r),
            )
            for r in order
        ]
        for copy in waits:
            copy.wait_recv()
        total = part_group[step, 0]
        for r in range(1, tiles):
            total = total + part_group[step, r]
        part_depth[step, 0] = total
        waits = [
            ship(
                part_depth.at[step, 0],
                part_depth.at[step, rd],
                part_send.at[step, tiles + rd],
                part_recv.at[step, tiles + rd],
                depth_at(rd),
            )
            for rd in range(1, n_depth)
        ]
        for copy in waits:
            copy.wait_recv()
        for rd in range(1, n_depth):
            total = total + part_depth[step, rd]
        total = jnp.broadcast_to(jnp.sum(total, axis=1, keepdims=True), total.shape)
        scalars = [total[q : q + 1, :] for q in range(2 * ITERS)]
        gram = [
            [scalars[i + j] - scalars[i + j + 1] for j in range(ITERS)] for i in range(ITERS)
        ]
        factors = solve_small(gram, scalars[:ITERS])
        for j in range(ITERS):
            pressure = pressure + factors[j] * fields[j]
            residual = residual - factors[j] * (diagonal * (fields[j] - fields[j + 1]))
        for copy in far:
            copy.wait_recv()
        for j in range(ITERS):
            term = factors[j] * krylov[step, j].reshape(tiles * cells, lanes)
            pressure_all = term if pressure_all is None else pressure_all + term
        felt = jnp.dot(
            one_hot_column,
            pressure_all,
            precision=HIGHEST,
            preferred_element_type=jnp.float32,
        )
        moved = jnp.zeros((grains, lanes), jnp.float32)
        for c in range(3):
            force = (normal_sums[c] * felt).reshape(grains, per_grain, lanes)
            force = jnp.sum(jnp.sum(force, axis=1), axis=1, keepdims=True)
            velocity[c] = velocity[c] + STEP_TIME * force / mass_ref[...]
            displace[c] = displace[c] + STEP_TIME * velocity[c]
            moved = jnp.where(lane == c, displace[c], moved)
    press_out[...] = pressure
    speed = jnp.zeros((grains, lanes), jnp.float32)
    for c in range(3):
        speed = jnp.where(lane == c, velocity[c], speed)
    speed_out[...] = speed
    for copy in sent:
        copy.wait_send()


def per_device(
    sizes,
    fluid_offsets,
    source,
    marker_offsets,
    marker_normals,
    dest_tile,
    cell_index,
    grain_velocity,
    grain_mass,
):
    n_flow, n_cross, n_depth = sizes
    tiles = n_flow * n_cross
    dims = source.shape[:3]
    cells = dims[0] * dims[1] * dims[2]
    lanes = source.shape[3]
    grains, per_grain = cell_index.shape
    blocks = grains * per_grain
    tile = dest_tile.reshape(blocks)
    slot_flow = (lax.axis_index("flow") - tile // n_cross) % n_flow
    slot_cross = (lax.axis_index("cross") - tile % n_cross) % n_cross
    slot = (slot_flow * n_cross + slot_cross).astype(jnp.int32)
    cell = cell_index.reshape(blocks)
    place = slot * cells + cell
    offsets = (fluid_offsets * SCALE).reshape(3 * cells, lanes)
    geometry = jnp.concatenate(
        [
            marker_offsets * SCALE,
            marker_normals,
            jnp.zeros((grains, per_grain, COLS - 6, lanes), jnp.float32),
        ],
        axis=2,
    ).reshape(grains, per_grain * COLS, lanes)
    start = jnp.pad(grain_velocity, ((0, 0), (0, lanes - 3)))
    mass = jnp.broadcast_to(grain_mass[:, None], (grains, lanes))
    near_count = len({1, n_depth - 1})
    vmem, dma = pltpu.VMEM, pltpu.SemaphoreType.DMA
    f32 = jnp.float32
    in_vmem = pl.BlockSpec(memory_space=pltpu.VMEM)
    in_smem = pl.BlockSpec(memory_space=pltpu.SMEM)
    pressure, speed = pl.pallas_call(
        functools.partial(kernel, sizes, dims),
        out_shape=(
            jax.ShapeDtypeStruct((cells, lanes), f32),
            jax.ShapeDtypeStruct((grains, lanes), f32),
        ),
        in_specs=[in_smem] * 2 + [in_vmem] * 7,
        out_specs=(in_vmem, in_vmem),
        scratch_shapes=[
            vmem((tiles, 3 * cells, lanes), f32),
            vmem((near_count, 3 * cells, lanes), f32),
            vmem((cells, 7, lanes, lanes), f32),
            vmem((grains, lanes, per_grain * COLS), f32),
            vmem((grains, lanes), f32),
            vmem((3, blocks, lanes), f32),
            vmem((STEPS, tiles, cells, lanes), f32),
            vmem((STEPS, tiles, cells, lanes), f32),
            vmem((STEPS, ITERS, tiles, cells, lanes), f32),
            vmem((STEPS, ITERS, near_count, cells, lanes), f32),
            vmem((STEPS, tiles, 2 * ITERS, lanes), f32),
            vmem((STEPS, n_depth, 2 * ITERS, lanes), f32),
            dma((tiles + near_count,)),
            dma((tiles + near_count,)),
            dma((STEPS, tiles)),
            dma((STEPS, tiles)),
            dma((STEPS, ITERS, tiles + near_count)),
            dma((STEPS, ITERS, tiles + near_count)),
            dma((STEPS, tiles + n_depth)),
            dma((STEPS, tiles + n_depth)),
        ],
        compiler_params=pltpu.CompilerParams(
            collective_id=0, has_side_effects=True, vmem_limit_bytes=56 * 1024 * 1024
        ),
        name="coupled",
    )(
        slot,
        cell,
        offsets,
        source.reshape(cells, lanes),
        geometry,
        start,
        mass,
        place[:, None],
        place[None, :],
    )
    return (pressure.reshape(source.shape), speed[:, :3])


def solution(mesh):
    sizes = tuple(mesh.shape[name] for name in ("flow", "cross", "depth"))
    return jax.shard_map(
        functools.partial(per_device, sizes),
        mesh=mesh,
        in_specs=(
            P(None, "flow", "cross", "depth", None),
            P("flow", "cross", "depth", None),
            P(("flow", "cross", "depth"), None, None, None),
            P(("flow", "cross", "depth"), None, None, None),
            P(("flow", "cross", "depth"), None, None),
            P(("flow", "cross", "depth"), None),
            P(("flow", "cross", "depth"), None),
            P(("flow", "cross", "depth")),
        ),
        out_specs=(P("flow", "cross", "depth", None), P(("flow", "cross", "depth"), None)),
        check_vma=False,
    )
```

```python
import functools
import math

import jax
import jax.numpy as jnp
from jax import lax
from jax.experimental import pallas as pl
from jax.experimental.pallas import tpu as pltpu
from jax.sharding import PartitionSpec as P

ITERS = 4
STEPS = 2
STIFFEN = 0.5
STEP_TIME = 0.05
PER_PARTICLE = 1.0 / 128.0
SCALE = math.sqrt(math.log2(math.e))
SHIFT = math.log2(PER_PARTICLE)
MESH = pl.DeviceIdType.MESH
HIGHEST = lax.Precision.HIGHEST
COLS = 8


def weight_of(gaps):
    total = None
    for gap in gaps:
        total = gap * gap if total is None else total + gap * gap
    return jnp.exp2(SHIFT - total)


def rounded(value):
    return value.astype(jnp.bfloat16).astype(jnp.float32)


def three_parts(value):
    high = rounded(value)
    middle = rounded(value - high)
    return high, middle, (value - high) - middle


def solve_small(gram, right):
    n = len(right)
    gram = [list(row) for row in gram]
    right = list(right)
    for i in range(n):
        inverse = 1.0 / gram[i][i]
        for j in range(i + 1, n):
            factor = gram[j][i] * inverse
            for k in range(i + 1, n):
                gram[j][k] = gram[j][k] - factor * gram[i][k]
            right[j] = right[j] - factor * right[i]
    out = [None] * n
    for i in reversed(range(n)):
        value = right[i]
        for k in range(i + 1, n):
            value = value - gram[i][k] * out[k]
        out[i] = value / gram[i][i]
    return out


def kernel(
    sizes,
    dims,
    slot_ref,
    cell_ref,
    off_ref,
    source_ref,
    geo_ref,
    start_ref,
    mass_ref,
    column_ref,
    row_ref,
    press_out,
    speed_out,
    off_group,
    off_depth,
    weights,
    geo_turned,
    own_features,
    shift_rows,
    normal_sums,
    give,
    take,
    krylov,
    krylov_depth,
    part_group,
    part_depth,
    off_send,
    off_recv,
    take_send,
    take_recv,
    kry_send,
    kry_recv,
    part_send,
    part_recv,
):
    n_flow, n_cross, n_depth = sizes
    size_x, size_y, size_z = dims
    cells = size_x * size_y * size_z
    tiles = n_flow * n_cross
    grains = geo_ref.shape[0]
    blocks = column_ref.shape[0]
    per_grain = blocks // grains
    lanes = off_ref.shape[-1]
    flow, cross, depth = (lax.axis_index("flow"), lax.axis_index("cross"), lax.axis_index("depth"))

    def group_at(slot):
        rf, rc = divmod(slot, n_cross)
        return (lax.rem(flow + rf, n_flow), lax.rem(cross + rc, n_cross), depth)

    def group_back(slot):
        rf, rc = divmod(slot, n_cross)
        return (
            lax.rem(flow + n_flow - rf, n_flow),
            lax.rem(cross + n_cross - rc, n_cross),
            depth,
        )

    def depth_at(rd):
        return (flow, cross, lax.rem(depth + rd, n_depth))

    slot_flow = {1: (n_flow - 1) * n_cross, -1: (1 % n_flow) * n_cross}
    slot_cross = {1: n_cross - 1, -1: 1 % n_cross}
    near_slots = sorted({slot_flow[1], slot_flow[-1], slot_cross[1], slot_cross[-1]} - {0})
    far_slots = [r for r in range(1, tiles) if r not in near_slots]
    near_slots = sorted(near_slots, key=lambda r: r // n_cross)
    order = near_slots + far_slots
    near_depth = sorted({1, n_depth - 1})
    depth_index = {1: near_depth.index(n_depth - 1), -1: near_depth.index(1)}

    barrier = pltpu.get_barrier_semaphore()
    for r in range(1, tiles):
        pl.semaphore_signal(barrier, inc=1, device_id=group_at(r), device_id_type=MESH)
    for rd in range(1, n_depth):
        pl.semaphore_signal(barrier, inc=1, device_id=depth_at(rd), device_id_type=MESH)
    pl.semaphore_wait(barrier, tiles - 1 + n_depth - 1)

    sent = []

    def ship(src, dst, send_sem, recv_sem, device):
        copy = pltpu.make_async_remote_copy(
            src_ref=src,
            dst_ref=dst,
            send_sem=send_sem,
            recv_sem=recv_sem,
            device_id=device,
            device_id_type=MESH,
        )
        copy.start()
        sent.append(copy)
        return copy

    off_copies = {}
    for r in order:
        off_copies[r] = ship(
            off_ref, off_group.at[r], off_send.at[r], off_recv.at[r], group_at(r)
        )
    off_depth_copies = []
    for i, rd in enumerate(near_depth):
        off_depth_copies.append(
            ship(
                off_ref,
                off_depth.at[i],
                off_send.at[tiles + i],
                off_recv.at[tiles + i],
                depth_at(rd),
            )
        )
    off_group[0] = off_ref[...]

    part = lax.rem(lax.broadcasted_iota(jnp.int32, (per_grain * COLS, lanes), 0), COLS)
    row = lax.broadcasted_iota(jnp.int32, (COLS, lanes), 0)
    block_lane = lax.broadcasted_iota(jnp.int32, (lanes, per_grain * COLS), 1) // COLS

    def turn(g, carry):
        rows = geo_ref[g]
        high = rounded(rows)
        low = rows - high
        low = jnp.concatenate([low[3:], low[:3]], axis=0)
        mix = jnp.where(part < 3, low, jnp.where(part < 6, high, 0.0))
        geo_turned[g] = jnp.transpose(mix)
        return carry

    def own_pass(slot, carry):
        done = []
        for cell in range(cells):
            own = [off_group[slot, c * cells + cell : c * cells + cell + 1, :] for c in range(3)]
            square = own[0] * own[0] + own[1] * own[1] + own[2] * own[2] - SHIFT
            base = jnp.where(row == 4, -square, 0.0)
            for c in range(3):
                base = jnp.where(row == c, 2.0 * own[c], base)
            high, middle, low = three_parts(base)
            high = jnp.where(row == 3, -1.0, high)
            features = jnp.concatenate([high, middle, low, high, middle, high], axis=0)
            done.append(jnp.transpose(features).astype(jnp.bfloat16))
        for cell in range(cells):
            own_features[slot * cells + cell] = done[cell]
        return carry

    lax.fori_loop(0, grains, turn, 0)
    for r in order:
        off_copies[r].wait_recv()
    lax.fori_loop(0, tiles, own_pass, 0)

    one_hot_row = (
        lax.broadcasted_iota(jnp.int32, (tiles * cells, blocks), 0) == row_ref[...]
    ).astype(jnp.float32)

    def marker_pass(g, carry):
        shift = shift_rows[g]
        turned = geo_turned[g]
        total = None
        for b in range(per_grain):
            place = slot_ref[g * per_grain + b] * cells + cell_ref[g * per_grain + b]
            point = jnp.where(row < 3, geo_ref[g, b * COLS : (b + 1) * COLS, :] + shift, 0.0)
            square = jnp.sum(point * point, axis=0, keepdims=True)
            point = jnp.where(row == 3, square, jnp.where(row == 4, 1.0, point))
            high, middle, low = three_parts(point)
            features = jnp.concatenate([high, high, high, middle, middle, low], axis=0)
            weight = jnp.exp2(
                jnp.dot(
                    own_features[place],
                    features.astype(jnp.bfloat16),
                    preferred_element_type=jnp.float32,
                )
            )
            upper = weight.astype(jnp.bfloat16)
            lower = (weight - upper.astype(jnp.float32)).astype(jnp.bfloat16)
            normals = jnp.where(block_lane == b, turned, 0.0).astype(jnp.bfloat16)
            term = jnp.dot(
                jnp.concatenate([upper, lower], axis=1),
                jnp.concatenate([normals, normals], axis=0),
                preferred_element_type=jnp.float32,
            )
            total = term if total is None else total + term
        total = jnp.transpose(total).reshape(per_grain, COLS, lanes)
        for c in range(3):
            normal_sums[c, pl.ds(pl.multiple_of(g * per_grain, 8), per_grain), :] = (
                total[:, c, :] + total[:, c + 3, :]
            )
        return carry

    lane = lax.rem(lax.broadcasted_iota(jnp.int32, (grains, lanes), 1), COLS)
    speed = start_ref[...]
    moved = jnp.zeros((grains, lanes), jnp.float32)
    velocity = [jnp.broadcast_to(speed[:, c : c + 1], (grains, lanes)) for c in range(3)]
    displace = [moved, moved, moved]

    def to_fluid(step):
        added = None
        for c in range(3):
            term = normal_sums[c].reshape(grains, per_grain, lanes) * velocity[c][:, None, :]
            added = term if added is None else added + term
        spread = jnp.dot(
            one_hot_row,
            added.reshape(blocks, lanes),
            precision=HIGHEST,
            preferred_element_type=jnp.float32,
        )
        give[step] = spread.reshape(tiles, cells, lanes)
        return [
            ship(
                give.at[step, r],
                take.at[step, r],
                take_send.at[step, r],
                take_recv.at[step, r],
                group_back(r),
            )
            for r in reversed(order)
        ]

    def collect(step, copies):
        total = give[step, 0]
        for copy in copies:
            copy.wait_recv()
        for r in range(1, tiles):
            total = total + take[step, r]
        return total

    merged = size_x == 1 and n_flow == 2
    sources = {("own", 0): 0}
    flow_keys = [("flow", 1)] if merged else [("flow", 1), ("flow", -1)]
    for key in flow_keys + [("cross", 1), ("cross", -1), ("depth", 1), ("depth", -1)]:
        sources[key] = len(sources)
    padded_rows = -(-len(sources) * cells // 128) * 128

    def columns_of(pick):
        rows = []
        for axis, side in sources:
            if axis == "own":
                rows.append(pick(0, None))
            elif axis == "flow":
                rows.append(pick(slot_flow[side], None))
            elif axis == "cross":
                rows.append(pick(slot_cross[side], None))
            else:
                rows.append(pick(None, depth_index[side]))
        spare = padded_rows - len(sources) * cells
        if spare:
            rows.append(jnp.zeros((spare, lanes), jnp.float32))
        return jnp.transpose(jnp.concatenate(rows, axis=0))

    def pairs(cell):
        x, rest = divmod(cell, size_y * size_z)
        y, z = divmod(rest, size_z)
        found = [(cell, (0, 0, 0))]
        place, extent, names = (x, y, z), (size_x, size_y, size_z), ("flow", "cross", "depth")
        for axis in range(3):
            for side in (1, -1):
                near = list(place)
                near[axis] += side
                key = ("own", 0)
                if not 0 <= near[axis] < extent[axis]:
                    near[axis] %= extent[axis]
                    key = (names[axis], side)
                    if axis == 0 and merged:
                        key = (names[axis], 1)
                index = (near[0] * size_y + near[1]) * size_z + near[2]
                step = [0, 0, 0]
                step[axis] = side
                found.append((sources[key] * cells + index, tuple(step)))
        return found

    groups = []
    for cell in range(cells):
        by_column = {}
        for column, step in pairs(cell):
            by_column.setdefault(column, []).append(step)
        groups.append(list(by_column.items()))

    shift_rows[...] = jnp.zeros(shift_rows.shape, jnp.float32)
    lax.fori_loop(0, grains, marker_pass, 0)
    copies = to_fluid(0)
    for copy in off_depth_copies:
        copy.wait_recv()

    turned = [
        columns_of(
            lambda slot, i, c=c: (
                off_group[slot, c * cells : (c + 1) * cells, :]
                if i is None
                else off_depth[i, c * cells : (c + 1) * cells, :]
            )
        )
        for c in range(3)
    ]
    sum_rows = []
    for cell in range(cells):
        own = [off_ref[c * cells + cell : c * cells + cell + 1, :] for c in range(3)]
        full = None
        for position, (column, steps) in enumerate(groups[cell]):
            total = None
            for step in steps:
                weight = weight_of(
                    [
                        turned[c][:, column : column + 1] - (own[c] - SCALE * step[c])
                        for c in range(3)
                    ]
                )
                total = weight if total is None else total + weight
            weights[cell, position] = total
            full = total if full is None else full + total
        sum_rows.append(jnp.sum(full, axis=0, keepdims=True))
    rowsum = jnp.concatenate(sum_rows, axis=0)
    diagonal = STIFFEN + rowsum - PER_PARTICLE
    inverse = 1.0 / diagonal

    def weighted(step, j):
        turned_field = columns_of(
            lambda slot, i: krylov[step, j, slot] if i is None else krylov_depth[step, j, i]
        )
        rows = []
        for cell in range(cells):
            total = None
            for low in range(0, lanes, 64):
                acc = None
                for position, (column, _) in enumerate(groups[cell]):
                    term = (
                        weights[cell, position, low : low + 64, :]
                        * turned_field[low : low + 64, column : column + 1]
                    )
                    acc = term if acc is None else acc + term
                acc = jnp.sum(acc.reshape(8, 8, lanes), axis=0)
                total = acc if total is None else total + acc
            rows.append(jnp.sum(total, axis=0, keepdims=True))
        return jnp.concatenate(rows, axis=0)

    pressure = jnp.zeros((cells, lanes), jnp.float32)
    spread_before = None
    residual = None
    pressure_all = None
    one_hot_column = (
        lax.broadcasted_iota(jnp.int32, (blocks, tiles * cells), 1) == column_ref[...]
    ).astype(jnp.float32)
    for step in range(STEPS):
        if step:
            shift = jnp.zeros(shift_rows.shape, jnp.float32)
            component = lax.broadcasted_iota(jnp.int32, shift_rows.shape, 1)
            for c in range(3):
                shift = jnp.where(component == c, SCALE * displace[c][:, None, :], shift)
            shift_rows[...] = shift
            lax.fori_loop(0, grains, marker_pass, 0)
            copies = to_fluid(step)
        spread = collect(step, copies)
        if step == 0:
            residual = source_ref[...] + spread
        else:
            residual = residual + (spread - spread_before)
        spread_before = spread
        fields = [residual * inverse]
        far = []
        for j in range(ITERS):
            krylov[step, j, 0] = fields[j]
            near = {}
            for r in near_slots:
                near[r] = ship(
                    krylov.at[step, j, 0],
                    krylov.at[step, j, r],
                    kry_send.at[step, j, r],
                    kry_recv.at[step, j, r],
                    group_at(r),
                )
            beside = [
                ship(
                    krylov.at[step, j, 0],
                    krylov_depth.at[step, j, i],
                    kry_send.at[step, j, tiles + i],
                    kry_recv.at[step, j, tiles + i],
                    depth_at(rd),
                )
                for i, rd in enumerate(near_depth)
            ]
            for r in far_slots:
                far.append(
                    ship(
                        krylov.at[step, j, 0],
                        krylov.at[step, j, r],
                        kry_send.at[step, j, r],
                        kry_recv.at[step, j, r],
                        group_at(r),
                    )
                )
            for copy in list(near.values()) + beside:
                copy.wait_recv()
            fields.append((weighted(step, j) - PER_PARTICLE * fields[j]) * inverse)
        moments = []
        for j in range(ITERS):
            scaled = diagonal * fields[j]
            moments.append(jnp.sum(scaled * fields[j], axis=0, keepdims=True))
            moments.append(jnp.sum(scaled * fields[j + 1], axis=0, keepdims=True))
        part_group[step, 0] = jnp.concatenate(moments, axis=0)
        waits = [
            ship(
                part_group.at[step, 0],
                part_group.at[step, r],
                part_send.at[step, r],
                part_recv.at[step, r],
                group_at(r),
            )
            for r in order
        ]
        for copy in waits:
            copy.wait_recv()
        total = part_group[step, 0]
        for r in range(1, tiles):
            total = total + part_group[step, r]
        part_depth[step, 0] = total
        waits = [
            ship(
                part_depth.at[step, 0],
                part_depth.at[step, rd],
                part_send.at[step, tiles + rd],
                part_recv.at[step, tiles + rd],
                depth_at(rd),
            )
            for rd in range(1, n_depth)
        ]
        for copy in waits:
            copy.wait_recv()
        for rd in range(1, n_depth):
            total = total + part_depth[step, rd]
        total = jnp.broadcast_to(jnp.sum(total, axis=1, keepdims=True), total.shape)
        scalars = [total[q : q + 1, :] for q in range(2 * ITERS)]
        gram = [
            [scalars[i + j] - scalars[i + j + 1] for j in range(ITERS)] for i in range(ITERS)
        ]
        factors = solve_small(gram, scalars[:ITERS])
        for j in range(ITERS):
            pressure = pressure + factors[j] * fields[j]
            residual = residual - factors[j] * (diagonal * (fields[j] - fields[j + 1]))
        for copy in far:
            copy.wait_recv()
        for j in range(ITERS):
            term = factors[j] * krylov[step, j].reshape(tiles * cells, lanes)
            pressure_all = term if pressure_all is None else pressure_all + term
        felt = jnp.dot(
            one_hot_column,
            pressure_all,
            precision=HIGHEST,
            preferred_element_type=jnp.float32,
        )
        for c in range(3):
            force = (normal_sums[c] * felt).reshape(grains, per_grain, lanes)
            force = jnp.sum(jnp.sum(force, axis=1), axis=1, keepdims=True)
            velocity[c] = velocity[c] + STEP_TIME * force / mass_ref[...]
            displace[c] = displace[c] + STEP_TIME * velocity[c]
    press_out[...] = pressure
    speed = jnp.zeros((grains, lanes), jnp.float32)
    for c in range(3):
        speed = jnp.where(lane == c, velocity[c], speed)
    speed_out[...] = speed
    for copy in sent:
        copy.wait_send()


def per_device(
    sizes,
    fluid_offsets,
    source,
    marker_offsets,
    marker_normals,
    dest_tile,
    cell_index,
    grain_velocity,
    grain_mass,
):
    n_flow, n_cross, n_depth = sizes
    tiles = n_flow * n_cross
    dims = source.shape[:3]
    cells = dims[0] * dims[1] * dims[2]
    lanes = source.shape[3]
    grains, per_grain = cell_index.shape
    blocks = grains * per_grain
    tile = dest_tile.reshape(blocks)
    slot_flow = (lax.axis_index("flow") - tile // n_cross) % n_flow
    slot_cross = (lax.axis_index("cross") - tile % n_cross) % n_cross
    slot = (slot_flow * n_cross + slot_cross).astype(jnp.int32)
    cell = cell_index.reshape(blocks)
    place = slot * cells + cell
    offsets = (fluid_offsets * SCALE).reshape(3 * cells, lanes)
    geometry = jnp.concatenate(
        [
            marker_offsets * SCALE,
            marker_normals,
            jnp.zeros((grains, per_grain, COLS - 6, lanes), jnp.float32),
        ],
        axis=2,
    ).reshape(grains, per_grain * COLS, lanes)
    start = jnp.pad(grain_velocity, ((0, 0), (0, lanes - 3)))
    mass = jnp.broadcast_to(grain_mass[:, None], (grains, lanes))
    near_count = len({1, n_depth - 1})
    vmem, dma = pltpu.VMEM, pltpu.SemaphoreType.DMA
    f32 = jnp.float32
    in_vmem = pl.BlockSpec(memory_space=pltpu.VMEM)
    in_smem = pl.BlockSpec(memory_space=pltpu.SMEM)
    pressure, speed = pl.pallas_call(
        functools.partial(kernel, sizes, dims),
        out_shape=(
            jax.ShapeDtypeStruct((cells, lanes), f32),
            jax.ShapeDtypeStruct((grains, lanes), f32),
        ),
        in_specs=[in_smem] * 2 + [in_vmem] * 7,
        out_specs=(in_vmem, in_vmem),
        scratch_shapes=[
            vmem((tiles, 3 * cells, lanes), f32),
            vmem((near_count, 3 * cells, lanes), f32),
            vmem((cells, 7, lanes, lanes), f32),
            vmem((grains, lanes, per_grain * COLS), f32),
            vmem((tiles * cells, lanes, 6 * COLS), jnp.bfloat16),
            vmem((grains, COLS, lanes), f32),
            vmem((3, blocks, lanes), f32),
            vmem((STEPS, tiles, cells, lanes), f32),
            vmem((STEPS, tiles, cells, lanes), f32),
            vmem((STEPS, ITERS, tiles, cells, lanes), f32),
            vmem((STEPS, ITERS, near_count, cells, lanes), f32),
            vmem((STEPS, tiles, 2 * ITERS, lanes), f32),
            vmem((STEPS, n_depth, 2 * ITERS, lanes), f32),
            dma((tiles + near_count,)),
            dma((tiles + near_count,)),
            dma((STEPS, tiles)),
            dma((STEPS, tiles)),
            dma((STEPS, ITERS, tiles + near_count)),
            dma((STEPS, ITERS, tiles + near_count)),
            dma((STEPS, tiles + n_depth)),
            dma((STEPS, tiles + n_depth)),
        ],
        compiler_params=pltpu.CompilerParams(
            collective_id=0, has_side_effects=True, vmem_limit_bytes=60 * 1024 * 1024
        ),
        name="coupled",
    )(
        slot,
        cell,
        offsets,
        source.reshape(cells, lanes),
        geometry,
        start,
        mass,
        place[:, None],
        place[None, :],
    )
    return (pressure.reshape(source.shape), speed[:, :3])


def solution(mesh):
    sizes = tuple(mesh.shape[name] for name in ("flow", "cross", "depth"))
    return jax.shard_map(
        functools.partial(per_device, sizes),
        mesh=mesh,
        in_specs=(
            P(None, "flow", "cross", "depth", None),
            P("flow", "cross", "depth", None),
            P(("flow", "cross", "depth"), None, None, None),
            P(("flow", "cross", "depth"), None, None, None),
            P(("flow", "cross", "depth"), None, None),
            P(("flow", "cross", "depth"), None),
            P(("flow", "cross", "depth"), None),
            P(("flow", "cross", "depth")),
        ),
        out_specs=(P("flow", "cross", "depth", None), P(("flow", "cross", "depth"), None)),
        check_vma=False,
    )
```
